32 devices in a mesh: row: 4 (over y, x), seq: 8 (over z, core).
Axes of the slice: x: 2, y: 2, z: 4, core: 2. Of those that a mesh axis runs over, the one named last changes fastest.
Arguments:
- inputs: bfloat16 [4, 1024, 768], P('row', 'seq'), may hold values from -6 to 6
- documents: int32 [4, 1024], P('row', 'seq'), may hold values from 0 to 3, never falling along the last dimension, each value on 1 to 768 neighbouring positions
- offsets: int32 [5, 12], replicated, may hold values from 0 to 11, as said below
- ln1_gain: float32 [768], replicated, may hold values from 0.1 to 1.9
- ln1_bias: float32 [768], replicated, may hold values from -0.5 to 0.5
- qkv_weight: bfloat16 [768, 2304], replicated, may hold values from -0.21875 to 0.21875
- out_weight: bfloat16 [768, 768], replicated, may hold values from -0.875 to 0.875
- ln2_gain: float32 [768], replicated, may hold values from 0.1 to 1.9
- ln2_bias: float32 [768], replicated, may hold values from -0.5 to 0.5
- up_weight: bfloat16 [768, 3072], replicated, may hold values from -0.21875 to 0.21875
- down_weight: bfloat16 [3072, 768], replicated, may hold values from -0.109375 to 0.109375
- cotangent: bfloat16 [4, 1024, 768], P('row', 'seq'), may hold values from -6 to 6
Outputs:
- outputs: bfloat16 [4, 1024, 768], P('row', 'seq')
- grad_inputs: bfloat16 [4, 1024, 768], P('row', 'seq')
- grad_ln1_gain: float32 [768], P('row')
- grad_ln1_bias: float32 [768], P('row')
- grad_qkv: float32 [768, 2304], P('row')
- grad_out: float32 [768, 768], P('row')
- grad_ln2_gain: float32 [768], P('row')
- grad_ln2_bias: float32 [768], P('row')
- grad_up: float32 [768, 3072], P('row')
- grad_down: float32 [3072, 768], P('row')
The draws below stay inside these ranges and needn't reach their ends.
Inputs may be any that keep to these rules, and one draw needn't show every extreme that they name: Row k of offsets gives the heads' offsets for pattern k, of rate 1, 2, 4, 6, 12 (k = 0 .. 4): each offset 0 .. rate - 1 is taken by 12 / rate heads.
All inputs are finite; a program needn't handle non-finite values.
Results may differ from the reference program's by a relative error of at most 0.013.
Values may be sent and summed in bfloat16 or wider, within the bound.
No kernel may reach another device: no remote copies, remote signals or barrier semaphores. Data moves between devices by JAX's collectives and lax.ppermute only.
A program may use at most 320 MiB of HBM per device.

```python
import math
import jax
import jax.numpy as jnp
import numpy as np
from jax import lax

HEADS = 12
HDIM = 64
FF = 3072
D = 768
LEN = 1024
ROWS = 4


def draw_offsets(key, part):
    rows_list = []
    for pattern_id, dilation in enumerate((1, 2, 4, 6, 12)):
        ordering = jax.random.permutation(jax.random.fold_in(key, pattern_id + 11), HEADS)
        rows_list.append(jnp.mod(ordering, dilation).astype(jnp.int32))
    return jnp.stack(rows_list)


def block_levels(stream_key, extent, shards, least, high):
    level, own = 1.0, jax.random.fold_in(stream_key, 6)
    for position, parts in shards:
        draws = jnp.exp(jax.random.uniform(jax.random.fold_in(own, position), (parts,), jnp.float32, least / len(shards), high / len(shards)))
        level = level * jnp.repeat(draws, extent[position] // parts).reshape([-1 if axis == position else 1 for axis in range(len(extent))])
    return level


def profile(number_of, total, limit, lean):
    weights = [(1 << 20) // math.isqrt(grade ** lean) + 1 for grade in range(2, number_of + 1)]
    spare, holding = total - limit - (number_of - 1), [1] * (number_of - 1)
    while spare > 0:
        movable = [i for i in range(number_of - 1) if holding[i] < limit]
        pool, budget = sum([weights[i] for i in movable]), spare
        for i in movable:
            extra = min(limit - holding[i], max(1, budget * weights[i] // pool), spare)
            holding[i] = holding[i] + extra
            spare = spare - extra
    return np.array([limit] + holding)


def ragged_sizes(own_key, amount, total, limit, skew):
    if amount == 2:
        one = jax.random.randint(own_key, (), max(1, total - limit), min(limit, total - 1) + 1)
        return jnp.stack([one, total - one])
    lengths = jnp.asarray(profile(amount, total, limit, skew), jnp.int32)
    twos = (amount - 1) // 2
    giver, taker = lengths[1:1 + 2 * twos:2], lengths[2:2 + 2 * twos:2]
    room = jnp.minimum(giver - 1, limit - taker)
    passed = jax.random.randint(jax.random.fold_in(own_key, 1), (twos,), 0, 1 << 20) % (room + 1)
    lengths = lengths.at[1:1 + 2 * twos:2].set(giver - passed).at[2:2 + 2 * twos:2].set(taker + passed)
    return lengths[jax.random.permutation(jax.random.fold_in(own_key, 2), amount)]


def normal_values(rng, shape, width, limit, cuts=(), kind=jnp.bfloat16):
    array = jax.random.normal(rng, shape, jnp.float32) * width
    if len(cuts) > 0:
        array = block_levels(rng, shape, cuts, -0.22, 0.18) * array
    return jnp.clip(array, min=-limit, max=limit).astype(kind)


def setup_inputs(seed: int = 0) -> dict:
    key_list = jax.random.split(jax.random.key(seed), 13)
    return {
        "inputs": normal_values(key_list[0], (ROWS, LEN, D), 1.0, 6.0, ((0, 4), (1, 8))),
        "documents": jax.vmap(lambda own: jnp.searchsorted(jnp.cumsum(ragged_sizes(own, 4, LEN, 3 * LEN // 4, 2)), jnp.arange(LEN), side="right"))(jax.random.split(key_list[1], ROWS)).reshape((ROWS, LEN)).astype(jnp.int32),
        "offsets": draw_offsets(jax.random.fold_in(key_list[12], 71), 0),
        "ln1_gain": jnp.clip(1.0 + 0.18 * jax.random.normal(key_list[3], (D,), jnp.float32), 0.1, 1.9),
        "ln1_bias": jnp.clip(jax.random.uniform(key_list[4], (D,), jnp.float32, -0.5, 0.5), -0.5, 0.5),
        "qkv_weight": normal_values(key_list[5], (D, 3 * D), D ** -0.5, 0.21875),
        "out_weight": normal_values(key_list[6], (D, D), (D // 16) ** -0.5, 0.875),
        "ln2_gain": jnp.clip(1.0 + 0.18 * jax.random.normal(key_list[7], (D,), jnp.float32), 0.1, 1.9),
        "ln2_bias": jnp.clip(jax.random.uniform(key_list[8], (D,), jnp.float32, -0.5, 0.5), -0.5, 0.5),
        "up_weight": normal_values(key_list[9], (D, FF), D ** -0.5, 0.21875),
        "down_weight": normal_values(key_list[10], (FF, D), FF ** -0.5, 0.109375),
        "cotangent": normal_values(key_list[11], (ROWS, LEN, D), 1.0, 6.0, ((0, 4), (1, 8))),
    }


reaches = (2048, 4096, 8192, 16384, 32768)
dilations = (1, 2, 4, 6, 12)
epsilon = 1e-05
masked_score = -1e+30
highest = lax.Precision.HIGHEST

@jax.custom_vjp
def low(v):
    return lax.optimization_barrier(v.astype(jnp.bfloat16)).astype(jnp.float32)

@jax.custom_vjp
def low_back(v):
    return v

def low_keep(v):
    return (low(v), None)

def low_pass(kept, grad):
    return (grad,)

def back_keep(v):
    return (v, None)

def back_low(kept, grad):
    return (low(grad),)
low.defvjp(low_keep, low_pass)
low_back.defvjp(back_keep, back_low)

def layer_norm(values, gain_vec, shift_vec):
    centered = values - lax.optimization_barrier(jnp.mean(values, axis=-1, keepdims=True))
    variance = lax.optimization_barrier(jnp.mean(centered * centered, axis=-1, keepdims=True))
    return centered * lax.rsqrt(variance + epsilon) * gain_vec + shift_vec

def unit_attention(packed):
    queries, key_rows, value_rows, positions, doc_ids, is_valid = packed
    raw_scores = jnp.einsum('qe,ke->qk', queries, key_rows, precision=highest) * HDIM ** (-0.5)
    raw_scores = low_back(raw_scores)
    allowed = is_valid[None, :] & (positions[None, :] <= positions[:, None]) & (doc_ids[None, :] == doc_ids[:, None])
    scores = jnp.where(allowed, raw_scores, masked_score)
    row_top = lax.optimization_barrier(jnp.max(scores, axis=-1, keepdims=True))
    log_total = jnp.log(lax.optimization_barrier(jnp.sum(jnp.exp(scores - row_top), axis=-1, keepdims=True))) + row_top
    probability = jnp.exp(scores - log_total)
    attended = jnp.dot(low(probability), value_rows, precision=highest)
    return (attended, log_total[:, 0])

def dilated(queries, key_rows, value_rows, doc_row, offset_row, reach_len, dilation):
    span_len = min(reach_len, LEN)
    segments = LEN // span_len
    slot_count = -(-span_len // dilation)
    slot_ids = jnp.arange(slot_count, dtype=jnp.int32)
    in_segment = offset_row[:, None] + dilation * slot_ids[None, :]
    is_valid = in_segment < span_len
    seg_starts = (jnp.arange(segments, dtype=jnp.int32) * span_len)[:, None, None]
    positions = seg_starts + jnp.minimum(in_segment, span_len - 1)[None]
    head_ids = jnp.arange(HEADS, dtype=jnp.int32)[None, :, None]
    unit_total = segments * HEADS
    query_units = queries[positions, head_ids].reshape(unit_total, slot_count, HDIM)
    key_units = key_rows[positions, head_ids].reshape(unit_total, slot_count, HDIM)
    value_units = value_rows[positions, head_ids].reshape(unit_total, slot_count, HDIM)
    doc_units = doc_row[positions].reshape(unit_total, slot_count)
    pos_units = jnp.broadcast_to(in_segment[None], (segments, HEADS, slot_count)).reshape(unit_total, slot_count)
    valid_units = jnp.broadcast_to(is_valid[None], (segments, HEADS, slot_count)).reshape(unit_total, slot_count)
    attended, log_totals = lax.map(jax.checkpoint(unit_attention), (query_units, key_units, value_units, pos_units, doc_units, valid_units))
    attended = low_back(attended)
    target = jnp.where(is_valid[None], positions, LEN)
    out_full = jnp.zeros((LEN + 1, HEADS, HDIM), jnp.float32).at[target, head_ids].set(attended.reshape(segments, HEADS, slot_count, HDIM))
    lse_full = jnp.full((LEN + 1, HEADS), masked_score, jnp.float32).at[target, head_ids].set(log_totals.reshape(segments, HEADS, slot_count))
    return (out_full[:LEN], lse_full[:LEN])

def forward_row(inputs_row, params, doc_row, offsets):
    gain_one, shift_one, weight_qkv, weight_out, gain_two, shift_two, weight_up, weight_down = params
    normed_one = low(layer_norm(inputs_row, gain_one, shift_one))
    packed = jnp.dot(normed_one, weight_qkv, precision=highest)
    queries = low(low_back(packed[:, :D])).reshape(LEN, HEADS, HDIM)
    key_rows = low(low_back(packed[:, D:2 * D])).reshape(LEN, HEADS, HDIM)
    value_rows = low(low_back(packed[:, 2 * D:])).reshape(LEN, HEADS, HDIM)
    out_list = []
    lse_list = []
    for pattern_id in range(len(reaches)):
        attended, log_totals = dilated(queries, key_rows, value_rows, doc_row, offsets[pattern_id], reaches[pattern_id], dilations[pattern_id])
        out_list.append(attended)
        lse_list.append(log_totals)
    lse_stack = jnp.stack(lse_list)
    row_top = lax.optimization_barrier(jnp.max(lse_stack, axis=0))
    log_norm = row_top + jnp.log(lax.optimization_barrier(jnp.sum(jnp.exp(lse_stack - row_top), axis=0)))
    mix_weights = jnp.exp(lse_stack - log_norm)
    mixed = lax.optimization_barrier(jnp.sum(mix_weights[..., None] * jnp.stack(out_list), axis=0))
    attended_low = low(mixed.reshape(LEN, D))
    branch = low_back(jnp.dot(attended_low, weight_out, precision=highest))
    middle = inputs_row + branch
    normed_two = low(layer_norm(middle, gain_two, shift_two))
    hidden_pre = low_back(jnp.dot(normed_two, weight_up, precision=highest))
    hidden = low(jax.nn.gelu(hidden_pre, approximate=False))
    down = low_back(jnp.dot(hidden, weight_down, precision=highest))
    return middle + down

def add_pair(first_item, second_item):
    return first_item + second_item

def reference(inputs, documents, offsets, ln1_gain, ln1_bias, qkv_weight, out_weight, ln2_gain, ln2_bias, up_weight, down_weight, cotangent):
    params = (ln1_gain.astype(jnp.float32), ln1_bias.astype(jnp.float32), qkv_weight.astype(jnp.float32), out_weight.astype(jnp.float32), ln2_gain.astype(jnp.float32), ln2_bias.astype(jnp.float32), up_weight.astype(jnp.float32), down_weight.astype(jnp.float32))

    def per_row(totals, row_data):
        row_inputs, row_docs, row_cot = row_data

        def run_row(values, weights):
            return forward_row(values, weights, row_docs, offsets)
        result, pullback = jax.vjp(run_row, row_inputs.astype(jnp.float32), params)
        grad_row, grad_params = pullback(row_cot.astype(jnp.float32))
        totals = jax.tree.map(add_pair, totals, grad_params)
        return (totals, (result.astype(jnp.bfloat16), grad_row.astype(jnp.bfloat16)))
    zero_grads = jax.tree.map(jnp.zeros_like, params)
    totals, (outputs, grad_inputs) = lax.scan(per_row, zero_grads, (inputs, documents, cotangent))
    return (outputs, grad_inputs, totals[0], totals[1], totals[2], totals[3], totals[4], totals[5], totals[6], totals[7])
```

```python
import functools

import jax
import jax.numpy as jnp
from jax import lax
from jax.experimental import pallas as pl
from jax.experimental.pallas import tpu as pltpu
from jax.sharding import PartitionSpec as P

reaches = (2048, 4096, 8192, 16384, 32768)
dilations = (1, 2, 4, 6, 12)
period = 12
doc_count = 4
epsilon = 1e-05
negative = -1e30
bf16 = jnp.bfloat16
f32 = jnp.float32


def layer_norm(values, gain_vec, shift_vec):
    centered = values - jnp.mean(values, axis=-1, keepdims=True)
    variance = jnp.mean(centered * centered, axis=-1, keepdims=True)
    return centered * lax.rsqrt(variance + epsilon) * gain_vec + shift_vec


def gelu_exact(values):
    return jax.nn.gelu(values, approximate=False)


def matmul(left, right):
    return jnp.dot(left, right, preferred_element_type=f32)


def matmul_t(left, right):
    return lax.dot_general(left, right, (((1,), (1,)), ((), ())), preferred_element_type=f32)


def token_sum(left, right):
    return lax.dot_general(left, right, (((0,), (0,)), ((), ())), preferred_element_type=f32)


def split3(values):
    first = lax.reduce_precision(values, 8, 7)
    rest = values - first
    second = lax.reduce_precision(rest, 8, 7)
    return first.astype(bf16), second.astype(bf16), (rest - second).astype(bf16)


def swap_seq(value, mask):
    count = lax.axis_size("seq")
    return lax.ppermute(value, "seq", [(s, s ^ mask) for s in range(count)])


def swap_row(value, even_mask, odd_mask):
    rows = lax.axis_size("row")
    count = lax.axis_size("seq")
    pairs = []
    for r in range(rows):
        for s in range(count):
            partner = r ^ (odd_mask if s % 2 else even_mask)
            pairs.append((r * count + s, partner * count + s))
    return lax.ppermute(value, ("row", "seq"), pairs)


def direct(count):
    return count <= 8


def gather_blocks(block):
    count = lax.axis_size("seq")
    if direct(count):
        parts = [block]
        for apart in range(1, count // 2):
            parts.append(swap_seq(block, 2 * apart))
        mine = jnp.stack(parts)
        other = swap_seq(mine, 1)
        return jnp.stack([mine, other], axis=1).reshape((count,) + block.shape)
    return lax.all_gather(block, "seq", axis=0)


def sum_chips(block):
    count = lax.axis_size("seq")
    chips = count // 2
    if not direct(count):
        groups = [list(range(0, count, 2)), list(range(1, count, 2))]
        return lax.psum(block.astype(f32), "seq", axis_index_groups=groups).astype(bf16)
    chip = lax.axis_index("seq") // 2
    height = block.shape[0] // chips
    total = lax.dynamic_slice_in_dim(block, chip * height, height, 0).astype(f32)
    for apart in range(1, chips):
        piece = lax.dynamic_slice_in_dim(block, (chip ^ apart) * height, height, 0)
        total = total + swap_seq(piece, 2 * apart).astype(f32)
    total = total.astype(bf16)
    parts = [total]
    for apart in range(1, chips):
        parts.append(swap_seq(total, 2 * apart))
    result = jnp.zeros_like(block)
    for apart in range(chips):
        result = lax.dynamic_update_slice_in_dim(result, parts[apart], (chip ^ apart) * height, 0)
    return result


def sum_rows(piece_of):
    rows = lax.axis_size("row")
    r = lax.axis_index("row")
    core = lax.axis_index("seq") % 2
    first = jnp.where(core == 0, 1, 2)
    second = jnp.where(core == 0, 2, 1)
    sent = jnp.concatenate([piece_of(r ^ first), piece_of(r ^ first ^ second)], axis=0)
    got = swap_row(sent.astype(bf16), 1, 2)
    height = got.shape[0] // 2
    onward = piece_of(r ^ second) + got[height:].astype(f32)
    got_two = swap_row(onward.astype(bf16), 2, 1)
    return (piece_of(r) + got[:height].astype(f32) + got_two.astype(f32)).astype(bf16)


def fold_pair(ref_value, head_bit, lanes):
    return jnp.where((lanes >= 64) == (head_bit == 1), ref_value, jnp.zeros_like(ref_value))


def forward_kernel(
    place_ref, q_ref, k_ref, v_ref, own_ref, all_ref, out_ref, lse_ref, bias_ref, *, tokens, chunk
):
    pairs = q_ref.shape[1] // 128
    length = k_ref.shape[0]
    chunks = length // chunk
    step = pl.program_id(0)
    me = place_ref[0]
    flip = place_ref[1]
    lanes = lax.broadcasted_iota(jnp.int32, (tokens, 128), 1)

    @pl.when(step == 0)
    def _():
        lse_ref[...] = jnp.zeros_like(lse_ref)
        row = lax.broadcasted_iota(jnp.int32, (tokens, tokens), 0)
        col = lax.broadcasted_iota(jnp.int32, (tokens, tokens), 1)
        for c in range(length // tokens):
            block = c ^ flip
            allowed = (block < me) | ((block == me) & (col <= row))
            bias_ref[:, c * tokens : (c + 1) * tokens] = jnp.where(allowed, 0.0, negative)

    def scores(left, pair, begin):
        right = jnp.concatenate(
            [k_ref[pl.ds(begin, chunk), pair * 128 : pair * 128 + 128], all_ref[pl.ds(begin, chunk), :]],
            axis=1,
        )
        return matmul_t(left, right)

    for pair in range(pairs):
        span = slice(pair * 128, pair * 128 + 128)
        q_pair = q_ref[:, span]
        outs = []
        for bit in range(2):
            left = jnp.concatenate([fold_pair(q_pair, bit, lanes), own_ref[pair * 2 + bit]], axis=1)

            def one(c, carry, left=left):
                top, total, acc = carry
                begin = c * chunk if isinstance(c, int) else pl.multiple_of(c * chunk, chunk)
                s = scores(left, pair, begin) + bias_ref[:, pl.ds(begin, chunk)]
                new_top = jnp.max(s, axis=1, keepdims=True)
                if top is not None:
                    new_top = jnp.maximum(top, new_top)
                p = jnp.exp(s - new_top)
                new_total = jnp.sum(p, axis=1, keepdims=True)
                new_acc = matmul(p.astype(bf16), v_ref[pl.ds(begin, chunk), span])
                if top is not None:
                    scale = jnp.exp(top - new_top)
                    new_total = new_total + scale * total
                    new_acc = new_acc + scale * acc
                return new_top, new_total, new_acc

            if chunks == 1:
                top, total, acc = one(0, (None, None, None))
            else:
                start = (
                    jnp.full((tokens, 1), 4 * negative, f32),
                    jnp.zeros((tokens, 1), f32),
                    jnp.zeros((tokens, 128), f32),
                )
                top, total, acc = lax.fori_loop(0, chunks, one, start)
            outs.append(acc / total)
            head = step * pairs * 2 + pair * 2 + bit
            lse_ref[...] = jnp.where(lanes == head, top + jnp.log(total), lse_ref[...])
        out_ref[:, span] = jnp.where(lanes < 64, outs[0], outs[1])


def backward_kernel(
    place_ref,
    q_own,
    k_own,
    v_own,
    d_own,
    q_all,
    k_all,
    v_all,
    d_all,
    own_q,
    own_d,
    own_k,
    own_v,
    feat_q,
    feat_k,
    dq_ref,
    dk_ref,
    dv_ref,
    left_a,
    left_b,
    left_c,
    left_d,
    acc_q,
    acc_k,
    acc_v,
    *,
    tokens,
):
    pairs = q_own.shape[1] // 128
    blocks = q_all.shape[0] // tokens
    me = place_ref[0]
    flip = place_ref[1]
    lanes = lax.broadcasted_iota(jnp.int32, (tokens, 128), 1)
    low = lanes < 64
    for pair in range(pairs):
        span = slice(pair * 128, pair * 128 + 128)
        for bit in range(2):
            rows = slice(bit * tokens, (bit + 1) * tokens)
            head = pair * 2 + bit
            left_a[pair, rows, :] = jnp.concatenate(
                [fold_pair(q_own[:, span], bit, lanes), own_q[head]], axis=1
            )
            left_b[pair, rows, :] = jnp.concatenate(
                [fold_pair(d_own[:, span], bit, lanes), own_d[head]], axis=1
            )
            left_c[pair, rows, :] = jnp.concatenate(
                [fold_pair(k_own[:, span], bit, lanes), own_k[head]], axis=1
            )
            left_d[pair, rows, :] = jnp.concatenate(
                [
                    fold_pair(v_own[:, span], bit, lanes),
                    jnp.broadcast_to(own_v[head], (tokens, own_v.shape[2])),
                ],
                axis=1,
            )
    acc_q[...] = jnp.zeros_like(acc_q)
    acc_k[...] = jnp.zeros_like(acc_k)
    acc_v[...] = jnp.zeros_like(acc_v)
    row = lax.broadcasted_iota(jnp.int32, (2 * tokens, tokens), 0) % tokens
    col = lax.broadcasted_iota(jnp.int32, (2 * tokens, tokens), 1)
    later_col = jnp.where(col <= row, 0.0, negative)
    later_row = jnp.where(row <= col, 0.0, negative)

    def select(both):
        return jnp.where(low, both[:tokens], both[tokens:])

    def query_step(j, _):
        begin = pl.multiple_of((j ^ flip) * tokens, tokens)
        at_diag = (j == me).astype(f32)
        feats = feat_k[pl.ds(begin, tokens), :]
        for pair in range(pairs):
            span = slice(pair * 128, pair * 128 + 128)
            k_blk = k_all[pl.ds(begin, tokens), span]
            v_blk = v_all[pl.ds(begin, tokens), span]
            s = matmul_t(left_a[pair], jnp.concatenate([k_blk, feats], axis=1))
            dp = matmul_t(left_b[pair], jnp.concatenate([v_blk, feats], axis=1))
            w = jnp.exp(s + later_col * at_diag)
            ds = (w * dp).astype(bf16)
            acc_q[:, span] += select(matmul(ds, k_blk))
        return 0

    def key_step(j, _):
        begin = pl.multiple_of((j ^ flip) * tokens, tokens)
        at_diag = (j == me).astype(f32)
        feats = feat_q[pl.ds(begin, tokens), :]
        for pair in range(pairs):
            span = slice(pair * 128, pair * 128 + 128)
            q_blk = q_all[pl.ds(begin, tokens), span]
            d_blk = d_all[pl.ds(begin, tokens), span]
            s = matmul_t(left_c[pair], jnp.concatenate([q_blk, feats], axis=1))
            dp = matmul_t(left_d[pair], jnp.concatenate([d_blk, feats], axis=1))
            w = jnp.exp(s + later_row * at_diag)
            ds = (w * dp).astype(bf16)
            acc_k[:, span] += select(matmul(ds, q_blk))
            acc_v[:, span] += select(matmul(w.astype(bf16), d_blk))
        return 0

    lax.fori_loop(0, me + 1, query_step, 0)
    lax.fori_loop(me, blocks, key_step, 0)
    dq_ref[...] = (acc_q[...] * 0.125).astype(bf16)
    dk_ref[...] = acc_k[...].astype(bf16)
    dv_ref[...] = acc_v[...].astype(bf16)


def attend(place, q, k_all, v_all, own, feats, group):
    tokens, width = q.shape
    length = k_all.shape[0]
    chunk = min(length, 1024)
    lanes = 128 * group
    steps = width // lanes
    feat = feats.shape[1]
    spec = pltpu.PrefetchScalarGridSpec(
        num_scalar_prefetch=1,
        grid=(steps,),
        in_specs=[
            pl.BlockSpec((tokens, lanes), lambda i, _: (0, i)),
            pl.BlockSpec((length, lanes), lambda i, _: (0, i)),
            pl.BlockSpec((length, lanes), lambda i, _: (0, i)),
            pl.BlockSpec((2 * group, tokens, feat), lambda i, _: (i, 0, 0)),
            pl.BlockSpec((length, feat), lambda i, _: (0, 0)),
        ],
        out_specs=[
            pl.BlockSpec((tokens, lanes), lambda i, _: (0, i)),
            pl.BlockSpec((tokens, 128), lambda i, _: (0, 0)),
        ],
        scratch_shapes=[pltpu.VMEM((tokens, length), f32)],
    )
    return pl.pallas_call(
        functools.partial(forward_kernel, tokens=tokens, chunk=chunk),
        grid_spec=spec,
        out_shape=[
            jax.ShapeDtypeStruct((tokens, width), f32),
            jax.ShapeDtypeStruct((tokens, 128), f32),
        ],
        name="attend",
    )(place, q, k_all, v_all, own, feats)


def attend_back(place, owns, alls, own_feats, feats, group):
    tokens, width = owns[0].shape
    length = alls[0].shape[0]
    lanes = 128 * group
    steps = width // lanes
    feat = feats[0].shape[1]
    full = 128 + feat
    own_spec = pl.BlockSpec((tokens, lanes), lambda i, _: (0, i))
    all_spec = pl.BlockSpec((length, lanes), lambda i, _: (0, i))
    head_spec = pl.BlockSpec((2 * group, tokens, feat), lambda i, _: (i, 0, 0))
    flat_spec = pl.BlockSpec((2 * group, 1, feat), lambda i, _: (i, 0, 0))
    feat_spec = pl.BlockSpec((length, feat), lambda i, _: (0, 0))
    spec = pltpu.PrefetchScalarGridSpec(
        num_scalar_prefetch=1,
        grid=(steps,),
        in_specs=[own_spec] * 4
        + [all_spec] * 4
        + [head_spec, head_spec, head_spec, flat_spec, feat_spec, feat_spec],
        out_specs=[own_spec] * 3,
        scratch_shapes=[pltpu.VMEM((group, 2 * tokens, full), bf16)] * 4
        + [pltpu.VMEM((tokens, lanes), f32)] * 3,
    )
    return pl.pallas_call(
        functools.partial(backward_kernel, tokens=tokens),
        grid_spec=spec,
        out_shape=[jax.ShapeDtypeStruct((tokens, width), bf16)] * 3,
        name="attend_back",
    )(place, *owns, *alls, *own_feats, *feats)


def log_counts(offsets, positions, row_len, spans, parts):
    heads = offsets.shape[1]
    finest = spans[0]
    classes = jnp.arange(period, dtype=jnp.int32)
    part_start = jnp.arange(parts, dtype=jnp.int32) * finest
    total = jnp.zeros((heads, positions.shape[0], parts, period), f32)
    for index, dilation in enumerate(dilations):
        offset = offsets[index][:, None]
        own_in = jnp.mod(positions[None, :] - offset, dilation) == 0
        key_in = jnp.mod(classes[None, :] - offset, dilation) == 0
        same = positions[:, None] // spans[index] == part_start[None, :] // spans[index]
        both = own_in[:, :, None, None] & key_in[:, None, None, :] & same[None, :, :, None]
        total = total + both.astype(f32)
    logs = jnp.where(total > 0, jnp.log(jnp.maximum(total, 1.0)), negative)
    logs = logs.reshape(heads, positions.shape[0], parts * period)
    high = lax.reduce_precision(logs, 8, 7)
    return high.astype(bf16), (logs - high).astype(bf16)


def shards(
    inputs,
    documents,
    offsets,
    ln1_gain,
    ln1_bias,
    qkv_weight,
    out_weight,
    ln2_gain,
    ln2_bias,
    up_weight,
    down_weight,
    cotangent,
):
    tokens = inputs.shape[1]
    width = inputs.shape[2]
    heads = offsets.shape[1]
    hidden_width = up_weight.shape[1]
    rows = lax.axis_size("row")
    share = width // rows
    count = lax.axis_size("seq")
    me = lax.axis_index("seq")
    core = me % 2
    row_len = tokens * count
    flip = me if direct(count) else jnp.zeros_like(me)
    place = jnp.stack([me, flip]).astype(jnp.int32)
    spans = [min(reach, row_len) for reach in reaches]
    parts = row_len // spans[0]
    group = width // 128 if row_len <= 1024 else 1

    x_low = inputs[0]
    doc_rows = jnp.zeros((16, width), bf16).at[0, :tokens].set(documents[0].astype(bf16))
    gathered = gather_blocks(jnp.concatenate([x_low, doc_rows], axis=0))
    x_all = gathered[:, :tokens].reshape(row_len, width)
    docs_all = gathered[:, tokens, :tokens].reshape(row_len).astype(jnp.int32)
    block_of = jnp.arange(count, dtype=jnp.int32) ^ flip
    pos_all = (block_of[:, None] * tokens + jnp.arange(tokens, dtype=jnp.int32)[None, :]).reshape(-1)
    pos_own = me * tokens + jnp.arange(tokens, dtype=jnp.int32)
    docs_own = documents[0]

    key_class = (pos_all // spans[0]) * period + pos_all % period
    class_hot = (key_class[:, None] == jnp.arange(parts * period)[None, :]).astype(bf16)
    doc_hot = (docs_all[:, None] == jnp.arange(doc_count)[None, :]).astype(bf16)
    ones_at = 2 * parts * period + doc_count
    lse_at = ones_at + 3
    delta_at = lse_at + 3 * heads
    used = delta_at + 3 * heads
    feat = -(-used // 128) * 128
    feat_base = jnp.concatenate(
        [
            class_hot,
            class_hot,
            doc_hot,
            jnp.ones((row_len, 3), bf16),
            jnp.zeros((row_len, feat - lse_at), bf16),
        ],
        axis=1,
    )
    high, low = log_counts(offsets, pos_own, row_len, spans, parts)
    doc_part = jnp.where(docs_own[:, None] == jnp.arange(doc_count)[None, :], 0.0, negative).astype(bf16)
    doc_part = jnp.broadcast_to(doc_part[None], (heads, tokens, doc_count))
    own_base = jnp.concatenate(
        [high, low, doc_part, jnp.zeros((heads, tokens, feat - ones_at), bf16)], axis=2
    )

    x_own = x_low.astype(f32)
    normed_one, norm_one_back = jax.vjp(layer_norm, x_own, ln1_gain, ln1_bias)
    normed_all = layer_norm(x_all.astype(f32), ln1_gain, ln1_bias).astype(bf16)
    q_all = (matmul(normed_all, qkv_weight[:, :width]) ).astype(bf16) * jnp.asarray(0.125, bf16)
    k_all = matmul(normed_all, qkv_weight[:, width : 2 * width]).astype(bf16)
    v_all = matmul(normed_all, qkv_weight[:, 2 * width :]).astype(bf16)
    own_at = (me ^ flip) * tokens

    def own_rows(value):
        if direct(count):
            return value[:tokens]
        return lax.dynamic_slice_in_dim(value, own_at, tokens, 0)

    q_own, k_own, v_own = own_rows(q_all), own_rows(k_all), own_rows(v_all)
    mixed, lse = attend(place, q_own, k_all, v_all, own_base, feat_base, group)
    lse = lse[:, :heads]

    attended = mixed.astype(bf16)
    middle = x_own + matmul(attended, out_weight)
    normed_two, norm_two_back = jax.vjp(layer_norm, middle, ln2_gain, ln2_bias)
    normed_two_low = normed_two.astype(bf16)
    hidden_pre = matmul(normed_two_low, up_weight)
    hidden, gelu_back = jax.vjp(gelu_exact, hidden_pre)
    hidden_low = hidden.astype(bf16)
    result = middle + matmul(hidden_low, down_weight)
    grad_result = cotangent[0]
    grad_hidden = matmul_t(grad_result, down_weight)
    grad_pre = gelu_back(grad_hidden)[0].astype(bf16)
    grad_normed_two = matmul_t(grad_pre, up_weight)
    grad_middle_part, grad_ln2_gain, grad_ln2_bias = norm_two_back(grad_normed_two)
    grad_middle = grad_result.astype(f32) + grad_middle_part
    grad_branch = grad_middle.astype(bf16)
    grad_mixed = matmul_t(grad_branch, out_weight)
    delta = jnp.sum((lax.reduce_precision(grad_mixed, 8, 7) * mixed).reshape(tokens, heads, width // heads), axis=-1)

    lse3 = jnp.stack(split3(lse), axis=2)
    delta3 = jnp.stack(split3(delta), axis=2)
    head_columns = jnp.concatenate(
        [lse3.reshape(tokens, 3 * heads), delta3.reshape(tokens, 3 * heads)], axis=1
    )
    head_columns = jnp.pad(head_columns, ((0, 0), (lse_at, feat - used)))
    grad_mixed_low = grad_mixed.astype(bf16)
    sent = jnp.concatenate([grad_mixed_low, head_columns], axis=1)
    gathered_back = gather_blocks(sent).reshape(row_len, width + feat)
    d_all = gathered_back[:, :width]
    feat_back = gathered_back[:, width:] + jnp.concatenate(
        [feat_base[:, :ones_at], jnp.zeros((row_len, feat - ones_at), bf16)], axis=1
    )
    own_q = own_base + jnp.pad(-jnp.moveaxis(lse3, 1, 0), ((0, 0), (0, 0), (ones_at, feat - lse_at)))
    own_d = jnp.pad(-jnp.moveaxis(delta3, 1, 0), ((0, 0), (0, 0), (ones_at, feat - lse_at)))
    column = jnp.arange(feat)[None, :]
    head = jnp.arange(heads)[:, None]
    pick_lse = jnp.where((column >= lse_at) & (column < delta_at) & ((column - lse_at) // 3 == head), -1.0, 0.0)
    pick_delta = jnp.where((column >= delta_at) & (column < used) & ((column - delta_at) // 3 == head), -1.0, 0.0)
    own_k = own_base + pick_lse[:, None, :].astype(bf16)
    own_v = pick_delta[:, None, :].astype(bf16)
    d_q, d_k, d_v = attend_back(
        place,
        (q_own, k_own, v_own, grad_mixed_low),
        (q_all, k_all, v_all, d_all),
        (own_q, own_d, own_k, own_v),
        (feat_back, feat_base),
        group,
    )
    grad_packed = jnp.concatenate([d_q, d_k, d_v], axis=1)
    grad_normed_one = matmul_t(grad_packed, qkv_weight)
    grad_source_part, grad_ln1_gain, grad_ln1_bias = norm_one_back(grad_normed_one)
    grad_inputs = (grad_middle + grad_source_part).astype(bf16)[None]

    def halves(value):
        half = value.shape[1] // 2
        mine = lax.dynamic_slice_in_dim(value, core * half, half, 1)
        theirs = lax.dynamic_slice_in_dim(value, (1 - core) * half, half, 1)
        return mine, theirs

    def stripes(value):
        cut = value.reshape(tokens, rows, 2, value.shape[1] // (2 * rows))
        mine = lax.dynamic_index_in_dim(cut, core, 2, keepdims=False)
        theirs = lax.dynamic_index_in_dim(cut, 1 - core, 2, keepdims=False)
        return mine.reshape(tokens, -1), theirs.reshape(tokens, -1)

    def pair_up(mine, theirs):
        got = swap_seq(jnp.concatenate(theirs, axis=1), 1)
        both = []
        cursor = 0
        for own, other in zip(mine, theirs):
            both.append(
                jnp.concatenate([own, got[:, cursor : cursor + other.shape[1]]], axis=0)
            )
            cursor += other.shape[1]
        return both

    def slice_of(value, index):
        extent = value.shape[1] // rows
        return lax.dynamic_slice_in_dim(value, index * extent, extent, 1)

    def vectors(first, second):
        return jnp.pad(jnp.stack([first, second], axis=1), ((0, 0), (0, 126)))

    pre_mine, pre_theirs = halves(grad_pre)
    branch_mine, branch_theirs = halves(grad_branch)
    hidden_mine, hidden_theirs = stripes(hidden_low)
    normed_two_pair, pre_pair, attended_pair, branch_pair, hidden_pair, result_pair = pair_up(
        (normed_two_low, pre_mine, attended, branch_mine, hidden_mine, grad_result),
        (normed_two_low, pre_theirs, attended, branch_theirs, hidden_theirs, grad_result),
    )
    ln2_vectors = vectors(grad_ln2_gain, grad_ln2_bias)

    def first_piece(index):
        up = token_sum(slice_of(normed_two_pair, index), pre_pair)
        out = token_sum(slice_of(attended_pair, index), branch_pair)
        down = token_sum(slice_of(hidden_pair, index), result_pair)
        vec = lax.dynamic_slice_in_dim(ln2_vectors, index * share, share, 0)
        folds = down.shape[0] // share
        return jnp.concatenate(
            [up, out] + [down[i * share : (i + 1) * share] for i in range(folds)] + [vec], axis=1
        )

    first_total = sum_chips(sum_rows(first_piece))

    packed_mine, packed_theirs = halves(grad_packed)
    (packed_pair,) = pair_up((packed_mine,), (packed_theirs,))
    if direct(count):
        normed_pair = normed_all[: 2 * tokens]
    else:
        normed_low = normed_one.astype(bf16)
        normed_pair = jnp.concatenate([normed_low, swap_seq(normed_low, 1)], axis=0)
    ln1_vectors = vectors(grad_ln1_gain, grad_ln1_bias)

    def second_piece(index):
        qkv = token_sum(slice_of(normed_pair, index), packed_pair)
        vec = lax.dynamic_slice_in_dim(ln1_vectors, index * share, share, 0)
        return jnp.concatenate([qkv, vec], axis=1)

    second_total = sum_chips(sum_rows(second_piece))

    def both_cores(mine):
        other = swap_seq(mine, 1)
        return jnp.where(core == 0, mine, other), jnp.where(core == 0, other, mine)

    even, odd = both_cores(first_total)
    up_half = hidden_width // 2
    out_half = width // 2
    up_end = up_half
    out_end = up_end + out_half
    folds = hidden_width // 2 // width
    down_end = out_end + folds * width
    grad_up = jnp.concatenate([even[:, :up_end], odd[:, :up_end]], axis=1).astype(f32)
    grad_out = jnp.concatenate([even[:, up_end:out_end], odd[:, up_end:out_end]], axis=1).astype(f32)
    grad_down = jnp.concatenate(
        [
            part[:, out_end + i * width : out_end + (i + 1) * width]
            for part in (even, odd)
            for i in range(folds)
        ],
        axis=0,
    ).astype(f32)
    ln2 = even[:, down_end : down_end + 2].astype(f32) + odd[:, down_end : down_end + 2].astype(f32)
    even, odd = both_cores(second_total)
    qkv_half = 3 * width // 2
    grad_qkv = jnp.concatenate([even[:, :qkv_half], odd[:, :qkv_half]], axis=1).astype(f32)
    ln1 = even[:, qkv_half : qkv_half + 2].astype(f32) + odd[:, qkv_half : qkv_half + 2].astype(f32)
    return (
        result.astype(bf16)[None],
        grad_inputs,
        ln1[:, 0],
        ln1[:, 1],
        grad_qkv,
        grad_out,
        ln2[:, 0],
        ln2[:, 1],
        grad_up,
        grad_down,
    )


def solution(mesh):
    placed = (
        P("row", "seq", None),
        P("row", "seq"),
        P(),
        P(),
        P(),
        P(),
        P(),
        P(),
        P(),
        P(),
        P(),
        P("row", "seq", None),
    )
    return jax.shard_map(
        shards,
        mesh=mesh,
        in_specs=placed,
        out_specs=(
            P("row", "seq", None),
            P("row", "seq", None),
            P("row"),
            P("row"),
            P("row", None),
            P("row", None),
            P("row"),
            P("row"),
            P("row", None),
            P("row", None),
        ),
        check_vma=False,
    )
```

```python
import functools

import jax
import jax.numpy as jnp
from jax import lax
from jax.experimental import pallas as pl
from jax.experimental.pallas import tpu as pltpu
from jax.sharding import PartitionSpec as P


reaches = (2048, 4096, 8192, 16384, 32768)
dilations = (1, 2, 4, 6, 12)
period = 12
doc_count = 4
epsilon = 1e-05
negative = -1e30
bf16 = jnp.bfloat16
f32 = jnp.float32


def layer_norm(values, gain_vec, shift_vec):
    centered = values - jnp.mean(values, axis=-1, keepdims=True)
    variance = jnp.mean(centered * centered, axis=-1, keepdims=True)
    return centered * lax.rsqrt(variance + epsilon) * gain_vec + shift_vec


def matmul(left, right):
    return jnp.dot(left, right, preferred_element_type=f32)


def matmul_t(left, right):
    return lax.dot_general(left, right, (((1,), (1,)), ((), ())), preferred_element_type=f32)


def token_sum(left, right):
    return lax.dot_general(left, right, (((0,), (0,)), ((), ())), preferred_element_type=f32)


def swap_seq(value, mask):
    count = lax.axis_size("seq")
    return lax.ppermute(value, "seq", [(s, s ^ mask) for s in range(count)])


def swap_row(value, even_mask, odd_mask):
    rows = lax.axis_size("row")
    count = lax.axis_size("seq")
    pairs = []
    for r in range(rows):
        for s in range(count):
            partner = r ^ (odd_mask if s % 2 else even_mask)
            pairs.append((r * count + s, partner * count + s))
    return lax.ppermute(value, ("row", "seq"), pairs)


def direct(count):
    return count == 8


def gather_blocks(block):
    count = lax.axis_size("seq")
    if not direct(count):
        return [[lax.all_gather(block, "seq", axis=0, tiled=True)]]
    mine = [block]
    for apart in range(1, count // 2):
        mine.append(swap_seq(block, 2 * apart))
    other = []
    for part in mine:
        other.append(swap_seq(part, 1))
    both = [part for pair in zip(mine, other) for part in pair]
    return [both[: count // 2], both[count // 2 :]]


def places(me, count):
    blocks = jnp.arange(count, dtype=jnp.int32)
    if not direct(count):
        return blocks
    return (blocks ^ me) % (count // 2)


def span_of(me, group, groups, blocks):
    size = blocks // groups
    return (me // size ^ group) * size, size


def sum_chips(block):
    count = lax.axis_size("seq")
    height = block.shape[0] // 2
    if not direct(count):
        groups = [list(range(0, count, 2)), list(range(1, count, 2))]
        total = lax.psum(block.astype(f32), "seq", axis_index_groups=groups).astype(bf16)
        return total[:height], total[height:], jnp.zeros((), jnp.int32)
    side = lax.axis_index("seq") // 2 % 2
    kept = lax.dynamic_slice_in_dim(block, side * height, height, 0)
    sent = lax.dynamic_slice_in_dim(block, (1 - side) * height, height, 0)
    part = (kept.astype(f32) + swap_seq(sent, 2).astype(f32)).astype(bf16)
    total = (part.astype(f32) + swap_seq(part, 4).astype(f32)).astype(bf16)
    other = swap_seq(total, 2)
    return total, other, side


def both_cores(halves, core):
    total, other, side = halves
    far_total = swap_seq(total, 1)
    far_other = swap_seq(other, 1)

    def pick(first, second, flag):
        return jnp.where(flag == 0, first, second), jnp.where(flag == 0, second, first)

    mine = jnp.concatenate(pick(total, other, side), axis=0)
    theirs = jnp.concatenate(pick(far_total, far_other, side), axis=0)
    return pick(mine, theirs, core)


def piece_kernel(*refs, count, windows, tokens, stripe):
    place_ref = refs[0]
    inputs = refs[1 : 1 + count]
    send_ref, onward_ref, own_ref = refs[1 + count : 4 + count]
    stripe_refs = refs[4 + count :]
    r, first, second = place_ref[0], place_ref[1], place_ref[2]
    share = own_ref.shape[0]

    def put(index, columns, value):
        apart = index ^ r

        @pl.when((apart == first) | (apart == 3))
        def _():
            slot = jnp.where(apart == 3, share, 0)
            send_ref[pl.ds(pl.multiple_of(slot, share), share), columns] = value.astype(bf16)

        @pl.when(apart == second)
        def _():
            onward_ref[:, columns] = value

        @pl.when(apart == 0)
        def _():
            own_ref[:, columns] = value

    for apart, target in enumerate(stripe_refs):
        begin, width = stripe
        lanes = pl.ds(pl.multiple_of(begin + (r ^ apart) * width, 128), width)
        target[:tokens, :] = inputs[0][:, lanes]
        target[tokens:, :] = inputs[1][:, lanes]
    at_column = 0
    for lefts, rights in windows:
        if rights is None:
            width = inputs[lefts].shape[1]
            for index in range(4):
                rows = slice(index * share, (index + 1) * share)
                put(index, slice(at_column, at_column + width), inputs[lefts][rows, :])
            at_column += width
            continue
        sources, begin, width = lefts
        left = jnp.concatenate([inputs[i][:, begin : begin + width] for i in sources], axis=0)
        sources, begin, width = rights
        for start in range(begin, begin + width, 384):
            right = jnp.concatenate([inputs[i][:, start : start + 384] for i in sources], axis=0)
            grads = token_sum(left, right)
            for index in range(4):
                rows = slice(index * share, (index + 1) * share)
                put(index, slice(at_column, at_column + 384), grads[rows])
            at_column += 384


def piece_call(inputs, windows, columns, share, tokens, stripe=None):
    r = lax.axis_index("row")
    core = lax.axis_index("seq") % 2
    place = jnp.stack([r, jnp.where(core == 0, 1, 2), jnp.where(core == 0, 2, 1)]).astype(jnp.int32)
    shape = jax.ShapeDtypeStruct
    outs = [shape((2 * share, columns), bf16)] + [shape((share, columns), f32)] * 2
    if stripe:
        outs += [shape((2 * tokens, stripe[1]), bf16)] * 4
    vmem = pl.BlockSpec(memory_space=pltpu.VMEM)
    return pl.pallas_call(
        functools.partial(
            piece_kernel, count=len(inputs), windows=windows, tokens=tokens, stripe=stripe
        ),
        in_specs=[pl.BlockSpec(memory_space=pltpu.SMEM)] + [vmem] * len(inputs),
        out_specs=[vmem] * len(outs),
        out_shape=outs,
        name="pieces",
        compiler_params=pltpu.CompilerParams(vmem_limit_bytes=20 << 20),
    )(place, *inputs)


def row_start(piece):
    send, onward, own = piece
    got = swap_row(send, 1, 2)
    height = onward.shape[0]
    return (onward + got[height:].astype(f32)).astype(bf16), own, got[:height]


def row_end(started):
    onward, own, got = [jnp.concatenate(items, axis=1) for items in zip(*started)]
    got_two = swap_row(onward, 2, 1)
    return (own + got.astype(f32) + got_two.astype(f32)).astype(bf16)


def when(condition):
    if isinstance(condition, bool):
        return lambda body: body() if condition else None
    return pl.when(condition)


def fold_pair(value, bit, lanes):
    return jnp.where((lanes >= 64) == (bit == 1), value, jnp.zeros_like(value))


def split_columns(column):
    first = column.astype(bf16).astype(f32)
    second = (column - first).astype(bf16).astype(f32)
    return first, second, column - first - second


def put_columns(array, lanes, at, columns, sign):
    for step, column in enumerate(columns):
        array = jnp.where(lanes == at + step, sign * column, array)
    return array


def vector_sums(upstream, z, lanes):
    ones = jnp.where(lanes == 0, 1.0, 0.0).astype(bf16)
    twos = jnp.where(lanes == 1, 1.0, 0.0).astype(bf16)
    return token_sum((upstream * z).astype(bf16), ones) + token_sum(upstream.astype(bf16), twos)


def project_kernel(*refs, tokens, partner):
    parts = refs[:-9] if partner else refs[:-8]
    gain_ref, shift_ref, weight_hbm, packed_ref, feats_ref = refs[len(parts) : len(parts) + 5]
    pair_ref, normed_ref, weight_ref, sems = refs[-4:]
    width = normed_ref.shape[1]
    copies = []
    for third in range(3):
        columns = pl.ds(third * width, width)
        copies.append(
            pltpu.make_async_copy(weight_hbm.at[:, columns], weight_ref.at[:, columns], sems.at[third])
        )
        copies[-1].start()
    for index, part in enumerate(parts):
        rows = slice(index * tokens, (index + 1) * tokens)
        x = part[:, :width].astype(f32)
        centered = x - jnp.mean(x, axis=1, keepdims=True)
        scale = lax.rsqrt(jnp.mean(centered * centered, axis=1, keepdims=True) + epsilon)
        normed = (centered * scale * gain_ref[...][None, :] + shift_ref[...][None, :]).astype(bf16)
        normed_ref[rows, :] = normed
        feats_ref[rows, :] = part[:, width:]
        if partner and index == 0:
            pair_ref[:tokens, :] = normed
        if partner and index == partner:
            pair_ref[tokens:, :] = normed
    for start in range(0, packed_ref.shape[1], 256):
        columns = slice(start, start + 256)
        if start % width == 0:
            copies[start // width].wait()
        packed_ref[:, columns] = matmul(normed_ref[...], weight_ref[:, columns]).astype(bf16)


def project_call(parts, gain, shift, weight, tokens, partner):
    count = len(parts)
    width, packed = weight.shape
    feat = parts[0].shape[1] - width
    shape = jax.ShapeDtypeStruct
    return pl.pallas_call(
        functools.partial(project_kernel, tokens=tokens, partner=partner),
        out_shape=[
            shape((count * tokens, packed), bf16),
            shape((count * tokens, feat), bf16),
        ]
        + ([shape((2 * tokens, width), bf16)] if partner else []),
        in_specs=[pl.BlockSpec(memory_space=pltpu.VMEM)] * (count + 2) + [pl.BlockSpec(memory_space=pl.ANY)],
        scratch_shapes=[
            pltpu.VMEM((count * tokens, width), bf16),
            pltpu.VMEM(weight.shape, bf16),
            pltpu.SemaphoreType.DMA((3,)),
        ],
        name="project",
        compiler_params=pltpu.CompilerParams(vmem_limit_bytes=16 << 20),
    )(*parts, gain, shift, weight)


def forward_kernel(*refs, tokens, chunk, groups, at, alone):
    place_ref, q_ref = refs[:2]
    k_refs = refs[2 : 2 + groups]
    v_refs = refs[2 + groups : 2 + 2 * groups]
    f_refs = refs[2 + 2 * groups : 2 + 3 * groups]
    own_ref, mine_ref, x_ref, cot_ref, gain_ref, shift_ref = refs[2 + 3 * groups : 8 + 3 * groups]
    out_hbm, up_hbm, down_hbm, result_ref, keep_ref, give_ref = refs[8 + 3 * groups : 14 + 3 * groups]
    middle_ref, send_ref, ownq_ref, ownd_ref, vec_ref = refs[14 + 3 * groups : 19 + 3 * groups]
    bias_ref, mixed_ref, cols_ref, out_w, up_w, down_w, sems = refs[19 + 3 * groups :]
    ones_at, lse_at, delta_at = at
    pairs = q_ref.shape[1] // 128
    length = k_refs[0].shape[0]
    chunks = length // chunk
    step, last = (0, 0) if alone else (pl.program_id(0), pl.num_programs(0) - 1)
    me = place_ref[0]
    core = me % 2
    feat = own_ref.shape[2]
    lanes = lax.broadcasted_iota(jnp.int32, (tokens, 128), 1)
    feat_lanes = lax.broadcasted_iota(jnp.int32, (tokens, feat), 1)
    copies = [
        pltpu.make_async_copy(out_hbm, out_w, sems.at[0]),
        pltpu.make_async_copy(up_hbm, up_w, sems.at[1]),
        pltpu.make_async_copy(down_hbm, down_w, sems.at[2]),
    ]

    @when(step == 0)
    def _():
        for copy in copies:
            copy.start()
        cols_ref[...] = mine_ref[...].astype(f32)
        row = lax.broadcasted_iota(jnp.int32, (tokens, tokens), 0)
        col = lax.broadcasted_iota(jnp.int32, (tokens, tokens), 1)
        blocks = groups * length // tokens
        for group in range(groups):
            begin, size = span_of(me, group, groups, blocks)
            for step_in in range(size):
                block = begin + step_in
                allowed = (block < me) | ((block == me) & (col <= row))
                place = pl.multiple_of(group * length + place_ref[1 + block] * tokens, tokens)
                bias_ref[:, pl.ds(place, tokens)] = jnp.where(allowed, 0.0, negative)

    for pair in range(pairs):
        span = slice(pair * 128, pair * 128 + 128)
        q_pair = q_ref[:, span] * jnp.asarray(0.125, bf16)
        outs = []
        for bit in range(2):
            left = jnp.concatenate([fold_pair(q_pair, bit, lanes), own_ref[pair * 2 + bit]], axis=1)

            def one(c, carry, left=left):
                top, total, acc = carry
                begin = c * chunk if isinstance(c, int) else pl.multiple_of(c * chunk, chunk)
                rows = pl.ds(begin, chunk)
                scores = []
                for group in range(groups):
                    right = jnp.concatenate([k_refs[group][rows, span], f_refs[group][rows, :]], axis=1)
                    shifted = pl.ds(group * length + begin, chunk)
                    scores.append(matmul_t(left, right) + bias_ref[:, shifted])
                tops = [jnp.max(s, axis=1, keepdims=True) for s in scores]
                new_top = functools.reduce(jnp.maximum, tops if top is None else [top] + tops)
                new_total = 0.0
                new_acc = 0.0
                for group, s in enumerate(scores):
                    p = jnp.exp(s - new_top)
                    new_total = new_total + jnp.sum(p, axis=1, keepdims=True)
                    new_acc = new_acc + matmul(p.astype(bf16), v_refs[group][rows, span])
                if top is not None:
                    scale = jnp.exp(top - new_top)
                    new_total = new_total + scale * total
                    new_acc = new_acc + scale * acc
                return new_top, new_total, new_acc

            if chunks == 1:
                top, total, acc = one(0, (None, None, None))
            else:
                start = (
                    jnp.full((tokens, 1), 4 * negative, f32),
                    jnp.zeros((tokens, 1), f32),
                    jnp.zeros((tokens, 128), f32),
                )
                top, total, acc = lax.fori_loop(0, chunks, one, start)
            outs.append(acc / total)
            head = step * pairs * 2 + pair * 2 + bit
            columns = split_columns(top + jnp.log(total))
            cols_ref[...] = put_columns(cols_ref[...], feat_lanes, lse_at + 3 * head, columns, 1.0)
            ownq_ref[pair * 2 + bit] = put_columns(
                own_ref[pair * 2 + bit].astype(f32), feat_lanes, ones_at, columns, -1.0
            ).astype(bf16)
        where = span
        if pairs * 128 < mixed_ref.shape[1]:
            where = pl.ds(pl.multiple_of(step * (pairs * 128) + pair * 128, 128), 128)
        mixed_ref[:, where] = jnp.where(lanes < 64, outs[0], outs[1])

    @when(step == last)
    def _():
        width = mixed_ref.shape[1]
        half = width // 2
        pieces = up_w.shape[1] // width
        up_half = up_w.shape[1] // 2
        cot = cot_ref[...]
        attended = mixed_ref[...].astype(bf16)
        copies[0].wait()
        middle = x_ref[...].astype(f32) + matmul(attended, out_w[...])
        centered = middle - jnp.mean(middle, axis=1, keepdims=True)
        scale = lax.rsqrt(jnp.mean(centered * centered, axis=1, keepdims=True) + epsilon)
        z = centered * scale
        normed = (z * gain_ref[...][None, :] + shift_ref[...][None, :]).astype(bf16)
        dU_at, att_at = width, width + up_half
        dB_at, hid_at = att_at + width, att_at + width + half
        cot_at = hid_at + up_half
        for ref in (keep_ref, give_ref):
            ref[:, :width] = normed
            ref[:, att_at : att_at + width] = attended
            ref[:, cot_at : cot_at + width] = cot
        copies[1].wait()
        copies[2].wait()
        y = middle
        grad_normed = jnp.zeros_like(middle)
        for c in range(pieces):
            cut = slice(c * width, (c + 1) * width)
            u = matmul(normed, up_w[:, cut])
            cdf = 0.5 + 0.5 * lax.erf(u * (0.5**0.5))
            hidden = (u * cdf).astype(bf16)
            slope = cdf + u * (jnp.exp(-0.5 * u * u) * 0.3989422804014327)
            grad_u = (matmul_t(cot, down_w[cut, :]) * slope).astype(bf16)
            y = y + matmul(hidden, down_w[cut, :])
            grad_normed = grad_normed + matmul_t(grad_u, up_w[:, cut])
            inner = slice(dU_at + (c % (pieces // 2)) * width, dU_at + (c % (pieces // 2) + 1) * width)
            stripe = slice(hid_at + c * half, hid_at + (c + 1) * half)

            @pl.when(core == c // (pieces // 2))
            def _(grad_u=grad_u, inner=inner):
                keep_ref[:, inner] = grad_u

            @pl.when(core != c // (pieces // 2))
            def _(grad_u=grad_u, inner=inner):
                give_ref[:, inner] = grad_u

            @pl.when(core == 0)
            def _(hidden=hidden, stripe=stripe):
                keep_ref[:, stripe] = hidden[:, :half]
                give_ref[:, stripe] = hidden[:, half:]

            @pl.when(core == 1)
            def _(hidden=hidden, stripe=stripe):
                keep_ref[:, stripe] = hidden[:, half:]
                give_ref[:, stripe] = hidden[:, :half]

        result_ref[...] = y.astype(bf16)
        vec_ref[...] = vector_sums(grad_normed, z, lanes)
        t = grad_normed * gain_ref[...][None, :]
        t_z = jnp.mean(t * z, axis=1, keepdims=True)
        grad_middle = cot.astype(f32) + scale * (t - jnp.mean(t, axis=1, keepdims=True) - z * t_z)
        middle_ref[...] = grad_middle
        branch = grad_middle.astype(bf16)
        grad_mixed = matmul_t(branch, out_w[...]).astype(bf16)
        send_ref[:, :width] = grad_mixed

        @pl.when(core == 0)
        def _():
            keep_ref[:, dB_at : dB_at + half] = branch[:, :half]
            give_ref[:, dB_at : dB_at + half] = branch[:, half:]

        @pl.when(core == 1)
        def _():
            keep_ref[:, dB_at : dB_at + half] = branch[:, half:]
            give_ref[:, dB_at : dB_at + half] = branch[:, :half]

        columns_all = cols_ref[...]
        for pair in range(width // 128):
            span = slice(pair * 128, pair * 128 + 128)
            product = grad_mixed[:, span].astype(f32) * mixed_ref[:, span]
            for bit in range(2):
                head = pair * 2 + bit
                delta = jnp.sum(fold_pair(product, bit, lanes), axis=1, keepdims=True)
                columns = split_columns(delta)
                columns_all = put_columns(columns_all, feat_lanes, delta_at + 3 * head, columns, 1.0)
                ownd_ref[head] = put_columns(
                    jnp.zeros((tokens, feat), f32), feat_lanes, ones_at, columns, -1.0
                ).astype(bf16)
        send_ref[:, width:] = columns_all.astype(bf16)


def stack_left(target, pair, value, bit, lanes, features):
    tokens = value.shape[0]
    target[pair, bit * tokens : (bit + 1) * tokens, :] = jnp.concatenate(
        [fold_pair(value, bit, lanes), features], axis=1
    )


def own_first(place_ref, me):
    return (place_ref[1 + me] < place_ref[1 + (me ^ 1)]).astype(jnp.int32)


def pair_rows(place_ref, j, tokens):
    first = jnp.minimum(place_ref[1 + 2 * j], place_ref[2 + 2 * j])
    return pl.ds(pl.multiple_of(first * tokens, 2 * tokens), 2 * tokens)


def pair_mask(tokens, me, swapped, first_own):
    shape = (2 * tokens, 2 * tokens)
    row = lax.broadcasted_iota(jnp.int32, shape, 0) % tokens
    col = lax.broadcasted_iota(jnp.int32, shape, 1)
    own_block = (col < tokens) == (first_own == 1)
    col = col % tokens
    if swapped:
        inside, beyond = row <= col, me % 2 == 0
    else:
        inside, beyond = col <= row, me % 2 == 1
    allowed = (own_block & inside) | (jnp.logical_not(own_block) & beyond)
    return jnp.where(allowed, 0.0, negative)


def query_kernel(*refs, tokens, groups, alone):
    place_ref, q_own, d_own, own_q, own_d = refs[:5]
    k_refs = refs[5 : 5 + groups]
    v_refs = refs[5 + groups : 5 + 2 * groups]
    f_refs = refs[5 + 2 * groups : 5 + 3 * groups]
    dq_ref, left_a, left_b, acc_q = refs[5 + 3 * groups :]
    pairs = q_own.shape[1] // 128
    blocks = groups * k_refs[0].shape[0] // tokens
    me = place_ref[0]
    lanes = lax.broadcasted_iota(jnp.int32, (tokens, 128), 1)
    low = lanes < 64
    for pair in range(pairs):
        span = slice(pair * 128, pair * 128 + 128)
        for bit in range(2):
            head = pair * 2 + bit
            stack_left(left_a, pair, q_own[:, span] * jnp.asarray(0.125, bf16), bit, lanes, own_q[head])
            stack_left(left_b, pair, d_own[:, span], bit, lanes, own_d[head])
    acc_q[...] = jnp.zeros_like(acc_q)
    later = pair_mask(tokens, me, False, own_first(place_ref, me))
    for group in range(groups):
        k_all, v_all, feat_k = k_refs[group], v_refs[group], f_refs[group]

        def query_step(j, _, k_all=k_all, v_all=v_all, feat_k=feat_k):
            rows = pair_rows(place_ref, j, tokens)
            at_diag = (j == me // 2).astype(f32)
            feats = feat_k[rows, :]
            for pair in range(pairs):
                span = slice(pair * 128, pair * 128 + 128)
                k_blk = k_all[rows, span]
                s = matmul_t(left_a[pair], jnp.concatenate([k_blk, feats], axis=1))
                dp = matmul_t(left_b[pair], jnp.concatenate([v_all[rows, span], feats], axis=1))
                ds = (jnp.exp(s + later * at_diag) * dp).astype(bf16)
                both = matmul(ds, k_blk)
                acc_q[:, span] += jnp.where(low, both[:tokens], both[tokens:])
            return 0

        begin, size = span_of(me, group, groups, blocks)
        end = jnp.minimum(begin + size, me // 2 * 2 + 2)
        lax.fori_loop(begin // 2, end // 2, query_step, 0)
    dq_ref[...] = (acc_q[...] * 0.125).astype(bf16)


def key_kernel(*refs, tokens, at, parts, group, groups, alone):
    final = group == groups - 1
    place_ref, k_own, v_own, q_all, own_base = refs[:5]
    given = refs[5 : 5 + parts]
    refs = refs[5 + parts :]
    if group > 0:
        k_before, v_before = refs[:2]
        refs = refs[2:]
    if final:
        wkv_hbm, start_ref, x_ref, gain_ref, middle_ref = refs[:5]
        keep_ref, give_ref, grad_ref, vec_ref = refs[5:9]
        acc_k, acc_v, wkv, sem, left_c, left_d = refs[9:15]
        refs = refs[15:]
    else:
        acc_k, acc_v, left_c, left_d = refs[:4]
        refs = refs[4:]
    _, lse_at, delta_at = at
    pairs = k_own.shape[1] // 128
    blocks = groups * q_all.shape[0] // tokens
    feat = own_base.shape[2]
    width = acc_k.shape[1]
    step, last = (0, 0) if alone else (pl.program_id(0), pl.num_programs(0) - 1)
    me = place_ref[0]
    core = me % 2
    lanes = lax.broadcasted_iota(jnp.int32, (tokens, 128), 1)
    feat_lanes = lax.broadcasted_iota(jnp.int32, (tokens, feat), 1)
    low = lanes < 64
    if final:
        copy = pltpu.make_async_copy(wkv_hbm.at[:, pl.ds(width, 2 * width)], wkv, sem)

        @when(step == 0)
        def _():
            copy.start()

    if parts == 2:
        d_all, feat_q = given
    else:
        d_all, feat_q = refs
        for index, part in enumerate(given):
            rows = slice(index * tokens, (index + 1) * tokens)
            d_all[rows, :] = part[:, :width]
            feat_q[rows, :] = part[:, width:]
    for pair in range(pairs):
        span = slice(pair * 128, pair * 128 + 128)
        for bit in range(2):
            head = pair * 2 + bit
            number = step * pairs * 2 + head
            minus = (jnp.full((tokens, 1), -1.0, f32),) * 3
            k_feats = put_columns(
                own_base[head].astype(f32), feat_lanes, lse_at + 3 * number, minus, 1.0
            ).astype(bf16)
            v_feats = put_columns(
                jnp.zeros((tokens, feat), f32), feat_lanes, delta_at + 3 * number, minus, 1.0
            ).astype(bf16)
            stack_left(left_c, pair, k_own[:, span] * jnp.asarray(0.125, bf16), bit, lanes, k_feats)
            stack_left(left_d, pair, v_own[:, span], bit, lanes, v_feats)

    def where(pair):
        if pairs * 128 == width:
            return slice(pair * 128, pair * 128 + 128)
        return pl.ds(pl.multiple_of(step * (pairs * 128) + pair * 128, 128), 128)

    for pair in range(pairs):
        if group > 0:
            acc_k[:, where(pair)] = k_before[:, where(pair)]
            acc_v[:, where(pair)] = v_before[:, where(pair)]
        else:
            acc_k[:, where(pair)] = jnp.zeros((tokens, 128), f32)
            acc_v[:, where(pair)] = jnp.zeros((tokens, 128), f32)
    later = pair_mask(tokens, me, True, own_first(place_ref, me))

    def key_step(j, _):
        rows = pair_rows(place_ref, j, tokens)
        at_diag = (j == me // 2).astype(f32)
        feats = feat_q[rows, :]
        for pair in range(pairs):
            span = slice(pair * 128, pair * 128 + 128)
            q_blk = q_all[rows, span]
            d_blk = d_all[rows, span]
            s = matmul_t(left_c[pair], jnp.concatenate([q_blk, feats], axis=1))
            dp = matmul_t(left_d[pair], jnp.concatenate([d_blk, feats], axis=1))
            w = jnp.exp(s + later * at_diag)
            both = matmul((w * dp).astype(bf16), q_blk)
            acc_k[:, where(pair)] += jnp.where(low, both[:tokens], both[tokens:])
            both = matmul(w.astype(bf16), d_blk)
            acc_v[:, where(pair)] += jnp.where(low, both[:tokens], both[tokens:])
        return 0

    begin, size = span_of(me, group, groups, blocks)
    lax.fori_loop(jnp.maximum(begin // 2, me // 2), (begin + size) // 2, key_step, 0)
    if not final:
        return

    @when(step == last)
    def _():
        d_k = (acc_k[...] * 0.125).astype(bf16)
        d_v = acc_v[...].astype(bf16)

        @pl.when(core == 0)
        def _():
            keep_ref[...] = d_k
            give_ref[...] = d_v

        @pl.when(core == 1)
        def _():
            keep_ref[...] = d_v
            give_ref[...] = d_k

        copy.wait()
        upstream = start_ref[...] + matmul_t(d_k, wkv[:, :width]) + matmul_t(d_v, wkv[:, width:])
        x = x_ref[...].astype(f32)
        centered = x - jnp.mean(x, axis=1, keepdims=True)
        scale = lax.rsqrt(jnp.mean(centered * centered, axis=1, keepdims=True) + epsilon)
        z = centered * scale
        vec_ref[...] = vector_sums(upstream, z, lanes)
        t = upstream * gain_ref[...][None, :]
        t_z = jnp.mean(t * z, axis=1, keepdims=True)
        grad = middle_ref[...] + scale * (t - jnp.mean(t, axis=1, keepdims=True) - z * t_z)
        grad_ref[...] = grad.astype(bf16)


class Plan:
    def __init__(self, tokens, length, width, feat, group):
        self.tokens, self.length, self.width, self.feat = tokens, length, width, feat
        self.lanes = 128 * group
        self.heads = 2 * group
        self.steps = width // self.lanes
        self.alone = self.steps == 1

    def own(self, third):
        block = (self.tokens, self.lanes)
        return block, lambda i, place: (place[1 + place[0]], third * self.steps + i), third * self.width

    def part(self):
        return (self.tokens, self.lanes), lambda i, place: (0, i), 0

    def all(self, third):
        block = (self.length, self.lanes)
        return block, lambda i, place: (0, third * self.steps + i), third * self.width

    def head(self):
        return (self.heads, self.tokens, self.feat), lambda i, place: (i, 0, 0), None

    def features(self):
        return (self.length, self.feat), lambda i, place: (0, 0), 0

    def own_features(self):
        return (self.tokens, self.feat), lambda i, place: (place[1 + place[0]], 0), 0

    def call(self, kernel, ins, outs, shapes, scratch, room):
        if not self.alone:
            kernel = functools.partial(kernel, alone=False)

            def spec(item):
                return pl.BlockSpec(item[0], item[1]) if isinstance(item, tuple) else item

            return pl.pallas_call(
                kernel,
                grid_spec=pltpu.PrefetchScalarGridSpec(
                    num_scalar_prefetch=1,
                    grid=(self.steps,),
                    in_specs=[spec(item) for item in ins],
                    out_specs=[spec(item) for item in outs],
                    scratch_shapes=scratch,
                ),
                out_shape=shapes,
            )

        vmem = pl.BlockSpec(memory_space=pltpu.VMEM)

        def run(place, *arrays):
            distinct, numbers, specs = [], [], []
            for item, array in zip(ins, arrays):
                same = [n for n, other in enumerate(distinct) if other is array]
                if not same:
                    same = [len(distinct)]
                    distinct.append(array)
                    specs.append(vmem if isinstance(item, tuple) else item)
                numbers.append(same[0])

            def body(place_ref, *refs):
                views = [place_ref]
                for item, number in zip(ins, numbers):
                    ref = refs[number]
                    if isinstance(item, tuple) and item[2] is not None:
                        block, _, begin = item
                        ref = ref.at[: block[0], begin : begin + block[1]]
                    views.append(ref)
                kernel(*views, *refs[len(distinct) :], alone=True)

            return pl.pallas_call(
                body,
                in_specs=[pl.BlockSpec(memory_space=pltpu.SMEM)] + specs,
                out_specs=[vmem] * len(outs),
                out_shape=shapes,
                scratch_shapes=scratch,
                compiler_params=pltpu.CompilerParams(vmem_limit_bytes=room << 20),
            )(place, *distinct)

        return run


def whole_spec(*shape):
    return shape, lambda i, place: (0,) * len(shape), None


def forward_call(plan, at, place, packed, own_base, feats, x, cot, gain, shift, weights):
    tokens, width, feat, groups = plan.tokens, plan.width, plan.feat, len(packed)
    out_weight, up_weight, down_weight = weights
    hidden = up_weight.shape[1]
    kept = 3 * width + width // 2 + hidden
    heads = plan.steps * plan.heads
    anywhere = pl.BlockSpec(memory_space=pl.ANY)
    shape = jax.ShapeDtypeStruct
    call = plan.call(
        functools.partial(
            forward_kernel, tokens=tokens, chunk=min(plan.length, 1024), groups=groups, at=at
        ),
        [plan.own(0)]
        + [plan.all(1)] * groups
        + [plan.all(2)] * groups
        + [plan.features()] * groups
        + [plan.head(), plan.own_features()]
        + [whole_spec(tokens, width)] * 2
        + [whole_spec(width)] * 2
        + [anywhere] * 3,
        [
            whole_spec(tokens, width),
            whole_spec(tokens, kept),
            whole_spec(tokens, kept),
            whole_spec(tokens, width),
            whole_spec(tokens, width + feat),
            plan.head(),
            whole_spec(heads, tokens, feat),
            whole_spec(width, 128),
        ],
        [
            shape((tokens, width), bf16),
            shape((tokens, kept), bf16),
            shape((tokens, kept), bf16),
            shape((tokens, width), f32),
            shape((tokens, width + feat), bf16),
            shape((heads, tokens, feat), bf16),
            shape((heads, tokens, feat), bf16),
            shape((width, 128), f32),
        ],
        [
            pltpu.VMEM((tokens, groups * plan.length), f32),
            pltpu.VMEM((tokens, width), f32),
            pltpu.VMEM((tokens, feat), f32),
            pltpu.VMEM(out_weight.shape, bf16),
            pltpu.VMEM(up_weight.shape, bf16),
            pltpu.VMEM(down_weight.shape, bf16),
            pltpu.SemaphoreType.DMA((3,)),
        ],
        30,
    )
    return call(
        place,
        packed[0],
        *packed,
        *packed,
        *feats,
        own_base,
        feats[0],
        x,
        cot,
        gain,
        shift,
        *weights,
    )


def query_call(plan, place, packed, sent, own_q, own_d, feats):
    tokens, lanes, full, groups = plan.tokens, plan.lanes, 128 + plan.feat, len(packed)
    group = plan.heads // 2
    call = plan.call(
        functools.partial(query_kernel, tokens=tokens, groups=groups),
        [plan.own(0), plan.part(), plan.head(), plan.head()]
        + [plan.all(1)] * groups
        + [plan.all(2)] * groups
        + [plan.features()] * groups,
        [plan.part()],
        [jax.ShapeDtypeStruct((tokens, plan.width), bf16)],
        [pltpu.VMEM((group, 2 * tokens, full), bf16)] * 2 + [pltpu.VMEM((tokens, lanes), f32)],
        14,
    )
    return call(place, packed[0], sent, own_q, own_d, *packed, *packed, *feats)[0]


def key_call(plan, at, place, packed, parts, own_base, group, groups, before, closing):
    tokens, width, full = plan.tokens, plan.width, 128 + plan.feat
    pairs = plan.heads // 2
    final = group == groups - 1
    shape = jax.ShapeDtypeStruct
    flat = whole_spec(tokens, width)
    left = [pltpu.VMEM((pairs, 2 * tokens, full), bf16)] * 2
    if len(parts) == 1:
        column = width // plan.feat
        features = ((plan.length, plan.feat), lambda i, place: (0, column), width)
        given, specs, more = parts * 2, [plan.all(0), features], []
    else:
        given, specs = parts, [whole_spec(tokens, width + plan.feat)] * len(parts)
        more = [pltpu.VMEM((plan.length, width), bf16), pltpu.VMEM((plan.length, plan.feat), bf16)]
    specs += [flat] * len(before)
    if final:
        specs += [pl.BlockSpec(memory_space=pl.ANY), flat, flat, whole_spec(width), flat]
        outs = [flat] * 3 + [whole_spec(width, 128)]
        shapes = [shape((tokens, width), bf16)] * 3 + [shape((width, 128), f32)]
        scratch = [pltpu.VMEM((tokens, width), f32)] * 2
        scratch += [pltpu.VMEM((width, 2 * width), bf16), pltpu.SemaphoreType.DMA]
    else:
        outs = [flat] * 2
        shapes = [shape((tokens, width), f32)] * 2
        scratch = []
    call = plan.call(
        functools.partial(
            key_kernel, tokens=tokens, at=at, parts=len(given), group=group, groups=groups
        ),
        [plan.own(1), plan.own(2), plan.all(0), plan.head()] + specs,
        outs,
        shapes,
        scratch + left + more,
        20,
    )
    return call(place, packed[0], packed[0], packed[group], own_base, *given, *before, *closing)


def log_counts(offsets, positions, spans, parts):
    heads = offsets.shape[1]
    finest = spans[0]
    classes = jnp.arange(period, dtype=jnp.int32)
    part_start = jnp.arange(parts, dtype=jnp.int32) * finest
    total = jnp.zeros((heads, positions.shape[0], parts, period), f32)
    for index, dilation in enumerate(dilations):
        offset = offsets[index][:, None]
        own_in = jnp.mod(positions[None, :] - offset, dilation) == 0
        key_in = jnp.mod(classes[None, :] - offset, dilation) == 0
        same = positions[:, None] // spans[index] == part_start[None, :] // spans[index]
        both = own_in[:, :, None, None] & key_in[:, None, None, :] & same[None, :, :, None]
        total = total + both.astype(f32)
    logs = jnp.where(total > 0, jnp.log(jnp.maximum(total, 1.0)), negative)
    logs = logs.reshape(heads, positions.shape[0], parts * period)
    high = lax.reduce_precision(logs, 8, 7)
    return high.astype(bf16), (logs - high).astype(bf16)


def shards(
    inputs,
    documents,
    offsets,
    ln1_gain,
    ln1_bias,
    qkv_weight,
    out_weight,
    ln2_gain,
    ln2_bias,
    up_weight,
    down_weight,
    cotangent,
):
    tokens = inputs.shape[1]
    width = inputs.shape[2]
    heads = offsets.shape[1]
    hidden_width = up_weight.shape[1]
    rows = lax.axis_size("row")
    share = width // rows
    count = lax.axis_size("seq")
    me = lax.axis_index("seq")
    core = me % 2
    row_len = tokens * count
    place = jnp.concatenate([me[None], places(me, count)]).astype(jnp.int32)
    spans = [min(reach, row_len) for reach in reaches]
    parts = row_len // spans[0]

    pos_own = me * tokens + jnp.arange(tokens, dtype=jnp.int32)
    docs_own = documents[0]
    ones_at = 2 * parts * period + doc_count
    lse_at = ones_at + 3
    delta_at = lse_at + 3 * heads
    used = delta_at + 3 * heads
    feat = -(-used // 128) * 128
    at = (ones_at, lse_at, delta_at)
    x_low = inputs[0]
    key_class = ((pos_own // spans[0]) * period + pos_own % period)[:, None]
    column = jnp.arange(feat, dtype=jnp.int32)[None, :]
    in_class = (column == key_class) | (column == key_class + parts * period)
    in_doc = column == docs_own[:, None] + 2 * parts * period
    hot = in_class | in_doc | ((column >= ones_at) & (column < lse_at))
    sent_first = jnp.concatenate([x_low, hot.astype(bf16)], axis=1)
    gathered = gather_blocks(sent_first)
    same_doc = docs_own[:, None] == jnp.arange(doc_count)[None, :]
    high, low = log_counts(offsets, pos_own, spans, parts)
    doc_part = jnp.where(same_doc, 0.0, negative).astype(bf16)
    doc_part = jnp.broadcast_to(doc_part[None], (heads, tokens, doc_count))
    own_base = jnp.concatenate(
        [high, low, doc_part, jnp.zeros((heads, tokens, feat - ones_at), bf16)], axis=2
    )

    cot = cotangent[0]
    cot_mine = [cot]
    for apart in range(1, rows):
        cot_mine.append(swap_row(cot, apart, apart))
    cot_other = swap_seq(jnp.concatenate(cot_mine, axis=0), 1)
    cot_all = jnp.concatenate(
        [
            part
            for apart, mine in enumerate(cot_mine)
            for part in (mine, cot_other[apart * tokens : (apart + 1) * tokens])
        ],
        axis=0,
    )

    if direct(count):
        packed_near, feats_near, normed_pair = project_call(
            gathered[0], ln1_gain, ln1_bias, qkv_weight, tokens, 1
        )
        packed_far, feats_far = project_call(gathered[1], ln1_gain, ln1_bias, qkv_weight, tokens, 0)
        packed, feats = [packed_near, packed_far], [feats_near, feats_far]
    else:
        ((joined,),) = gathered
        normed_all = layer_norm(joined[:, :width].astype(f32), ln1_gain, ln1_bias).astype(bf16)
        packed = [matmul(normed_all, qkv_weight).astype(bf16)]
        feats = [joined[:, width:]]
        normed_low = lax.dynamic_slice_in_dim(normed_all, me * tokens, tokens, 0)
        normed_pair = jnp.concatenate([normed_low, swap_seq(normed_low, 1)], axis=0)
    groups = len(packed)
    plan = Plan(tokens, row_len // groups, width, feat, width // 128 if row_len <= 1024 else 1)
    result, kept, given, grad_middle, sent, own_q, own_d, ln2_vectors = forward_call(
        plan,
        at,
        place,
        packed,
        own_base,
        feats,
        x_low,
        cot,
        ln2_gain,
        ln2_bias,
        (out_weight, up_weight, down_weight),
    )
    gathered_back = gather_blocks(sent)

    half = width // 2
    folds = hidden_width // 2 // width
    got = swap_seq(given, 1)
    up_half = hidden_width // 2
    attended_at = width + up_half
    branch_at = attended_at + width
    hidden_at = branch_at + half
    up_columns = up_half + half + 128
    pieces = piece_call(
        [kept, got, ln2_vectors],
        (
            (((0, 1), 0, width), ((0, 1), width, up_half)),
            (((0, 1), attended_at, width), ((0, 1), branch_at, half)),
            (2, None),
        ),
        up_columns,
        share,
        tokens,
        (hidden_at, half),
    )
    up_piece, stripes = pieces[:3], list(pieces[3:])
    for apart in range(1, rows):
        stripes[apart] = swap_row(stripes[apart], apart, apart)
    down = token_sum(jnp.concatenate(stripes, axis=0), cot_all)
    down = jnp.concatenate([down[i * share : (i + 1) * share] for i in range(folds)], axis=1)
    down_total = both_cores(sum_chips(down.astype(bf16)), core)

    up_started = row_start(up_piece)

    d_q = query_call(plan, place, packed, sent, own_q, own_d, feats)
    q_mine = lax.dynamic_slice_in_dim(d_q, core * half, half, 1)
    q_theirs = lax.dynamic_slice_in_dim(d_q, (1 - core) * half, half, 1)
    q_got = swap_seq(q_theirs, 1)
    start = matmul_t(d_q, qkv_weight[:, :width])
    query_piece = piece_call(
        [q_mine, q_got, normed_pair],
        ((((2,), 0, width), ((0, 1), 0, half)),),
        half,
        share,
        tokens,
    )
    query_started = row_start(query_piece)
    up_total = both_cores(sum_chips(row_end([up_started, query_started])), core)

    before = ()
    for group in range(groups):
        closing = ()
        if group == groups - 1:
            closing = (qkv_weight, start, x_low, ln1_gain, grad_middle)
        before = key_call(
            plan,
            at,
            place,
            packed,
            gathered_back[group],
            own_base,
            group,
            groups,
            tuple(before),
            closing,
        )
    kv_mine, kv_theirs, grad_inputs, ln1_vectors = before
    kv_got = swap_seq(kv_theirs, 1)
    kv_piece = piece_call(
        [kv_mine, kv_got, normed_pair, ln1_vectors],
        ((((2,), 0, width), ((0, 1), 0, width)), (3, None)),
        width + 128,
        share,
        tokens,
    )
    kv_total = both_cores(sum_chips(row_end([row_start(kv_piece)])), core)

    def columns(pair, begin, end):
        return jnp.concatenate([part[:, begin:end] for part in pair], axis=1).astype(f32)

    def vector(pair, at_column):
        first, second = [part[:, at_column : at_column + 2].astype(f32) for part in pair]
        return first + second

    grad_down = jnp.concatenate(
        [part[:, i * width : (i + 1) * width] for part in down_total for i in range(folds)], axis=0
    ).astype(f32)
    up_end = hidden_width // 2
    out_end = up_end + half
    vec_end = out_end + 128
    grad_up = columns(up_total, 0, up_end)
    grad_out = columns(up_total, up_end, out_end)
    ln2 = vector(up_total, out_end)
    grad_qkv = jnp.concatenate(
        [columns(up_total, vec_end, vec_end + half), columns(kv_total, 0, width)], axis=1
    )
    ln1 = vector(kv_total, width)
    return (
        result[None],
        grad_inputs[None],
        ln1[:, 0],
        ln1[:, 1],
        grad_qkv,
        grad_out,
        ln2[:, 0],
        ln2[:, 1],
        grad_up,
        grad_down,
    )


def solution(mesh):
    placed = (
        P("row", "seq", None),
        P("row", "seq"),
        P(),
        P(),
        P(),
        P(),
        P(),
        P(),
        P(),
        P(),
        P(),
        P("row", "seq", None),
    )

    return jax.shard_map(
        shards,
        mesh=mesh,
        in_specs=placed,
        out_specs=(
            P("row", "seq", None),
            P("row", "seq", None),
            P("row"),
            P("row"),
            P("row", None),
            P("row", None),
            P("row"),
            P("row"),
            P("row", None),
            P("row", None),
        ),
        check_vma=False,
    )
```
